32 devices in a mesh: groups: 2 (over x), seq: 16 (over z, y, core).
Axes of the slice: x: 2, y: 2, z: 4, core: 2. Of those that a mesh axis runs over, the one named last changes fastest.
Arguments:
- video_qkv: bfloat16 [4, 1536, 3, 4096], P('groups', 'seq'), parts along dimension 0, may hold values from -48 to 48
- video_cross_q: bfloat16 [4, 1536, 4096], P('groups', 'seq'), parts along dimension 0, may hold values from -48 to 48
- audio_kv_v: bfloat16 [4, 512, 2, 4096], P('groups', 'seq'), parts along dimension 0, may hold values from -4 to 4
- audio_qkv: bfloat16 [4, 512, 3, 2048], P('groups', 'seq'), parts along dimension 0, may hold values from -48 to 48
- audio_cross_q: bfloat16 [4, 512, 2048], P('groups', 'seq'), parts along dimension 0, may hold values from -48 to 48
- video_kv_a: bfloat16 [4, 1536, 2, 2048], P('groups', 'seq'), parts along dimension 0, may hold values from -4 to 4
- audio_valid: int32 [4], P('groups'), parts along dimension 0, may hold values from 256 to 512, as said below
- branch_prompt: int32 [4], P('groups'), parts along dimension 0, may hold values from 0 to 3
- video_gate: float32 [4, 4096], replicated, may hold values from 0.5 to 1.5
- audio_gate: float32 [4, 2048], replicated, may hold values from 0.5 to 1.5
Outputs:
- video_out: bfloat16 [4, 1536, 4096], P('groups', 'seq'), parts along dimension 0
- audio_out: bfloat16 [4, 512, 2048], P('groups', 'seq'), parts along dimension 0
The draws below stay inside these ranges and needn't reach their ends.
There are 2 independent parts, one for each index of `groups`. The reference program is written for one: setup_inputs(seed, part) draws one part's arguments, and reference() takes and returns one part's arrays. A program takes and returns all parts, laid end to end along the dimension named above; an argument that names none is the same for every part. Nothing has to cross between parts.
Inputs may be any that keep to these rules, and one draw needn't show every extreme that they name: `audio_valid`: at least one branch has all 512 audio tokens valid.
All inputs are finite; a program needn't handle non-finite values.
Results may differ from the reference program's by a relative error of at most 0.0058.
Values may be sent and summed in bfloat16 or wider, within the bound.
A program may use at most 128 MiB of HBM per device.

```python
import jax
import jax.numpy as jnp
from jax import lax

DV = 4096
HV = 32
DA = 2048
HA = 16
BR = 2
PROMPTS = 4
SV = 1536
SA = 512


def drawn_noise(key, marker, array_shape):
    return jnp.clip(jax.random.normal(jax.random.fold_in(key, marker), array_shape, jnp.float32), -4.0, 4.0)


def draw_video_qkv(key, part):
    noise = drawn_noise(key, 1, (BR, SV, 3, DV))
    return noise.astype(jnp.bfloat16)


def draw_video_cross_q(key, part):
    noise = drawn_noise(key, 2, (BR, SV, DV))
    return noise.astype(jnp.bfloat16)


def draw_audio_kv_v(key, part):
    noise = drawn_noise(key, 3, (BR, SA, 2, DV))
    return noise.astype(jnp.bfloat16)


def draw_audio_qkv(key, part):
    noise = drawn_noise(key, 4, (BR, SA, 3, DA))
    return noise.astype(jnp.bfloat16)


def draw_audio_cross_q(key, part):
    noise = drawn_noise(key, 5, (BR, SA, DA))
    return noise.astype(jnp.bfloat16)


def draw_video_kv_a(key, part):
    noise = drawn_noise(key, 6, (BR, SV, 2, DA))
    return noise.astype(jnp.bfloat16)


def draw_audio_valid(key, part):
    counts = jax.random.randint(jax.random.fold_in(key, 21), (BR,), SA // 2, SA + 1)
    full_branch = jax.random.randint(jax.random.fold_in(key, 22), (), 0, BR)
    return jnp.where(jnp.arange(BR) == full_branch, SA, counts).astype(jnp.int32)


def setup_inputs(seed: int = 0, part: int = 0) -> dict:
    arg_keys = jax.random.split(jax.random.key(seed), 11)
    part_keys = jax.random.split(jax.random.fold_in(arg_keys[10], part), 11)
    video_qkv = draw_video_qkv(jax.random.fold_in(jax.random.fold_in(arg_keys[10], part), 71), part)
    video_cross_q = draw_video_cross_q(jax.random.fold_in(jax.random.fold_in(arg_keys[10], part), 71), part)
    audio_kv_v = draw_audio_kv_v(jax.random.fold_in(jax.random.fold_in(arg_keys[10], part), 71), part)
    audio_qkv = draw_audio_qkv(jax.random.fold_in(jax.random.fold_in(arg_keys[10], part), 71), part)
    audio_cross_q = draw_audio_cross_q(jax.random.fold_in(jax.random.fold_in(arg_keys[10], part), 71), part)
    video_kv_a = draw_video_kv_a(jax.random.fold_in(jax.random.fold_in(arg_keys[10], part), 71), part)
    audio_valid = draw_audio_valid(jax.random.fold_in(jax.random.fold_in(arg_keys[10], part), 71), part)
    branch_prompt = jax.random.randint(part_keys[7], (BR,), 0, PROMPTS).astype(jnp.int32)
    video_gate = jnp.clip(jax.random.uniform(arg_keys[8], (PROMPTS, DV), jnp.float32, 0.5, 1.5), 0.5, 1.5)
    audio_gate = jnp.clip(jax.random.uniform(arg_keys[9], (PROMPTS, DA), jnp.float32, 0.5, 1.5), 0.5, 1.5)
    return {"video_qkv": video_qkv, "video_cross_q": video_cross_q, "audio_kv_v": audio_kv_v, "audio_qkv": audio_qkv, "audio_cross_q": audio_cross_q, "video_kv_a": video_kv_a, "audio_valid": audio_valid, "branch_prompt": branch_prompt, "video_gate": video_gate, "audio_gate": audio_gate}


def attend(queries, key_rows, value_rows, allowed):
    scores = jnp.dot(queries, key_rows.T, preferred_element_type=jnp.float32) * (queries.shape[-1] ** -0.5)
    if allowed is not None:
        scores = jnp.where(allowed[None, :], scores, -jnp.inf)
    row_max = jnp.max(scores, axis=1, keepdims=True)
    weights = jnp.exp(scores - row_max)
    shares = (weights / jnp.sum(weights, axis=1, keepdims=True)).astype(jnp.bfloat16)
    return jnp.dot(shares, value_rows, preferred_element_type=jnp.float32).astype(jnp.bfloat16)


def to_items(source, head_count):
    lead_count, row_count = source.shape[0], source.shape[1]
    middle = source.shape[2:-1]
    head_width = source.shape[-1] // head_count
    result = source.reshape((lead_count, row_count) + middle + (head_count, head_width))
    axes_order = (0, len(middle) + 2, 1) + tuple(range(2, len(middle) + 2)) + (len(middle) + 3,)
    result = jnp.transpose(result, axes_order)
    return result.reshape((lead_count * head_count, row_count) + middle + (head_width,))


def from_items(source, head_count):
    item_count, row_count, head_width = source.shape
    result = source.reshape(item_count // head_count, head_count, row_count, head_width)
    return jnp.transpose(result, (0, 2, 1, 3)).reshape(item_count // head_count, row_count, head_count * head_width)


def self_items(packed):
    return attend(packed[:, 0], packed[:, 1], packed[:, 2], None)


def self_masked(packed):
    return attend(packed[0][:, 0], packed[0][:, 1], packed[0][:, 2], packed[1])


def cross_masked(packed):
    return attend(packed[0], packed[1][:, 0], packed[1][:, 1], packed[2])


def cross_items(packed):
    return attend(packed[0], packed[1][:, 0], packed[1][:, 1], None)


def reference(video_qkv, video_cross_q, audio_kv_v, audio_qkv, audio_cross_q, video_kv_a, audio_valid, branch_prompt, video_gate, audio_gate):
    allowed = jnp.arange(SA, dtype=jnp.int32)[None, :] < audio_valid[:, None]
    video_self = lax.map(self_items, to_items(video_qkv, HV))
    video_cross = lax.map(cross_masked, (to_items(video_cross_q, HV), to_items(audio_kv_v, HV), jnp.repeat(allowed, HV, axis=0)))
    audio_self = lax.map(self_masked, (to_items(audio_qkv, HA), jnp.repeat(allowed, HA, axis=0)))
    audio_cross = lax.map(cross_items, (to_items(audio_cross_q, HA), to_items(video_kv_a, HA)))
    chosen = (branch_prompt[:, None] == jnp.arange(PROMPTS, dtype=jnp.int32)[None, :]).astype(jnp.float32)
    video_gates = jnp.dot(chosen, video_gate, precision=lax.Precision.HIGHEST)
    audio_gates = jnp.dot(chosen, audio_gate, precision=lax.Precision.HIGHEST)
    video_out = from_items(video_self, HV).astype(jnp.float32) + video_gates[:, None, :] * from_items(video_cross, HV).astype(jnp.float32)
    audio_out = from_items(audio_self, HA).astype(jnp.float32) + audio_gates[:, None, :] * from_items(audio_cross, HA).astype(jnp.float32)
    return video_out.astype(jnp.bfloat16), audio_out.astype(jnp.bfloat16)
```

```python
import functools

import jax
import jax.numpy as jnp
from jax import lax
from jax.experimental import pallas as pl
from jax.experimental.pallas import tpu as pltpu
from jax.sharding import PartitionSpec as P

HV = 32
HA = 16
HEAD = 128
PROMPTS = 4
MESH = pl.DeviceIdType.MESH


def attend(queries, key_rows, value_rows, bias):
    scores = lax.dot_general(
        queries, key_rows, (((1,), (1,)), ((), ())), preferred_element_type=jnp.float32
    ) * (HEAD**-0.5)
    if bias is not None:
        scores = scores + bias
    row_max = jnp.max(scores, axis=1, keepdims=True)
    weights = jnp.exp(scores - row_max)
    total = jnp.sum(weights, axis=1, keepdims=True)
    result = jnp.dot(
        weights.astype(jnp.bfloat16), value_rows, preferred_element_type=jnp.float32
    )
    return (result / total).astype(jnp.bfloat16).astype(jnp.float32)


def block_kernel(
    n,
    video_count,
    audio_count,
    video_block,
    audio_block,
    video_qkv,
    video_q,
    audio_kv,
    audio_qkv,
    audio_q,
    video_kv,
    video_gates,
    audio_gates,
    bias,
    video_out,
    audio_out,
    video_qkv_in,
    video_q_in,
    audio_kv_in,
    audio_qkv_in,
    audio_q_in,
    video_kv_in,
    video_res,
    audio_res,
    video_sems,
    audio_sems,
    send_sems,
    back_sems,
):
    me = lax.axis_index("seq")
    group = lax.axis_index("groups")
    video_local = video_out.shape[1]
    audio_local = audio_out.shape[1]

    barrier = pltpu.get_barrier_semaphore()

    def greet(k, carry):
        peer = lax.rem(me + k, n)
        pl.semaphore_signal(barrier, inc=1, device_id=(group, peer), device_id_type=MESH)
        return carry

    lax.fori_loop(1, n, greet, 0)
    pl.semaphore_wait(barrier, n - 1)

    video_rows = pl.ds(pl.multiple_of(me * video_local, video_local), video_local)
    audio_rows = pl.ds(pl.multiple_of(me * audio_local, audio_local), audio_local)

    def columns(head):
        return pl.ds(pl.multiple_of(head * HEAD, HEAD), HEAD)

    def video_parts(item, slot):
        branch, head = item // HV, lax.rem(item, HV)
        return (
            (video_qkv.at[item], video_qkv_in.at[slot, :, video_rows], video_sems.at[slot, 0]),
            (
                video_q.at[branch, :, columns(head)],
                video_q_in.at[slot, video_rows],
                video_sems.at[slot, 1],
            ),
            (audio_kv.at[item], audio_kv_in.at[slot, :, audio_rows], video_sems.at[slot, 2]),
        )

    def audio_parts(item, slot):
        branch, head = item // HA, lax.rem(item, HA)
        return (
            (audio_qkv.at[item], audio_qkv_in.at[slot, :, audio_rows], audio_sems.at[slot, 0]),
            (
                audio_q.at[branch, :, columns(head)],
                audio_q_in.at[slot, audio_rows],
                audio_sems.at[slot, 1],
            ),
            (video_kv.at[item], video_kv_in.at[slot, :, video_rows], audio_sems.at[slot, 2]),
        )

    def send(parts, count, slot, first_sem):
        def to_peer(k, carry):
            peer = lax.rem(me + k, n)
            for place, (source, target, sem) in enumerate(parts(peer * count + slot, slot)):
                pltpu.make_async_remote_copy(
                    src_ref=source,
                    dst_ref=target,
                    send_sem=send_sems.at[first_sem + place],
                    recv_sem=sem,
                    device_id=(group, peer),
                    device_id_type=MESH,
                ).start()
            return carry

        lax.fori_loop(1, n, to_peer, 0)
        for source, target, sem in parts(me * count + slot, slot):
            pltpu.make_async_copy(source, target, sem).start()

    def send_video(slot, carry):
        send(video_parts, video_count, slot, 0)
        return carry

    def send_audio(slot, carry):
        send(audio_parts, audio_count, slot, 3)
        return carry

    lax.fori_loop(0, video_count, send_video, 0)
    lax.fori_loop(0, audio_count, send_audio, 0)

    def settle(ref, sem):
        pltpu.make_async_copy(ref, ref, sem).wait()

    def give_back(result, slot, out, branch, head, local, first, count, place):
        def to_peer(j, carry):
            peer = first + j
            source = result.at[slot, pl.ds(pl.multiple_of(peer * local, local), local)]
            target = out.at[branch, :, columns(head)]

            @pl.when(peer == me)
            def _():
                pltpu.make_async_copy(source, target, back_sems.at[place]).start()

            @pl.when(peer != me)
            def _():
                pltpu.make_async_remote_copy(
                    src_ref=source,
                    dst_ref=target,
                    send_sem=send_sems.at[6 + place],
                    recv_sem=back_sems.at[place],
                    device_id=(group, peer),
                    device_id_type=MESH,
                ).start()

            return carry

        lax.fori_loop(0, count, to_peer, 0)

    def video_item(slot, carry):
        item = me * video_count + slot
        branch, head = item // HV, lax.rem(item, HV)
        settle(video_qkv_in.at[slot], video_sems.at[slot, 0])
        settle(video_q_in.at[slot], video_sems.at[slot, 1])
        settle(audio_kv_in.at[slot], video_sems.at[slot, 2])
        block = video_block * video_local

        def rows(i, inner):
            here = pl.ds(pl.multiple_of(i * block, block), block)
            own = attend(
                video_qkv_in[slot, 0, here], video_qkv_in[slot, 1], video_qkv_in[slot, 2], None
            )
            cross = attend(
                video_q_in[slot, here], audio_kv_in[slot, 0], audio_kv_in[slot, 1], bias[branch]
            )
            video_res[slot, here] = (own + video_gates[item] * cross).astype(jnp.bfloat16)
            give_back(
                video_res, slot, video_out, branch, head, video_local, i * video_block,
                video_block, 0,
            )
            return inner

        lax.fori_loop(0, n // video_block, rows, 0)
        return carry

    def audio_item(slot, carry):
        item = me * audio_count + slot
        branch, head = item // HA, lax.rem(item, HA)
        settle(audio_qkv_in.at[slot], audio_sems.at[slot, 0])
        settle(audio_q_in.at[slot], audio_sems.at[slot, 1])
        settle(video_kv_in.at[slot], audio_sems.at[slot, 2])
        block = audio_block * audio_local

        def rows(i, inner):
            here = pl.ds(pl.multiple_of(i * block, block), block)
            own = attend(
                audio_qkv_in[slot, 0, here],
                audio_qkv_in[slot, 1],
                audio_qkv_in[slot, 2],
                bias[branch],
            )
            cross = attend(
                audio_q_in[slot, here], video_kv_in[slot, 0], video_kv_in[slot, 1], None
            )
            audio_res[slot, here] = (own + audio_gates[item] * cross).astype(jnp.bfloat16)
            give_back(
                audio_res, slot, audio_out, branch, head, audio_local, i * audio_block,
                audio_block, 1,
            )
            return inner

        lax.fori_loop(0, n // audio_block, rows, 0)
        return carry

    lax.fori_loop(0, video_count, video_item, 0)
    lax.fori_loop(0, audio_count, audio_item, 0)

    far_video = pl.ds(0, (n - 1) * video_local)
    far_audio = pl.ds(0, (n - 1) * audio_local)
    settle(video_qkv_in.at[:, :, far_video], send_sems.at[0])
    settle(video_q_in.at[:, far_video], send_sems.at[1])
    settle(audio_kv_in.at[:, :, far_audio], send_sems.at[2])
    settle(audio_qkv_in.at[:, :, far_audio], send_sems.at[3])
    settle(audio_q_in.at[:, far_audio], send_sems.at[4])
    settle(video_kv_in.at[:, :, far_video], send_sems.at[5])
    settle(video_res.at[:, far_video], send_sems.at[6])
    settle(audio_res.at[:, far_audio], send_sems.at[7])
    settle(video_out, back_sems.at[0])
    settle(audio_out, back_sems.at[1])


def by_items(source, head_count):
    branches, rows, kinds, width = source.shape
    result = source.reshape(branches, rows, kinds, head_count, width // head_count)
    return jnp.transpose(result, (0, 3, 2, 1, 4)).reshape(
        branches * head_count, kinds, rows, width // head_count
    )


def on_device(
    n,
    video_qkv,
    video_cross_q,
    audio_kv_v,
    audio_qkv,
    audio_cross_q,
    video_kv_a,
    audio_valid,
    branch_prompt,
    video_gate,
    audio_gate,
):
    branches, video_local = video_cross_q.shape[:2]
    audio_local = audio_cross_q.shape[1]
    video_all, audio_all = video_local * n, audio_local * n
    video_count, audio_count = branches * HV // n, branches * HA // n
    positions = jnp.arange(audio_all, dtype=jnp.int32)
    bias = jnp.where(positions[None, :] < audio_valid[:, None], 0.0, -jnp.inf).astype(jnp.float32)
    chosen = (branch_prompt[:, None] == jnp.arange(PROMPTS, dtype=jnp.int32)[None, :]).astype(
        jnp.float32
    )
    video_gates = jnp.dot(chosen, video_gate, precision=lax.Precision.HIGHEST)
    audio_gates = jnp.dot(chosen, audio_gate, precision=lax.Precision.HIGHEST)
    hbm = pl.BlockSpec(memory_space=pl.ANY)
    vmem = pl.BlockSpec(memory_space=pltpu.VMEM)
    half = jnp.bfloat16
    return tuple(
        pl.pallas_call(
            functools.partial(
                block_kernel, n, video_count, audio_count, min(4, n), min(8, n)
            ),
            out_shape=(
                jax.ShapeDtypeStruct(video_cross_q.shape, half),
                jax.ShapeDtypeStruct(audio_cross_q.shape, half),
            ),
            in_specs=[hbm] * 6 + [vmem] * 3,
            out_specs=(hbm, hbm),
            scratch_shapes=[
                pltpu.VMEM((video_count, 3, video_all, HEAD), half),
                pltpu.VMEM((video_count, video_all, HEAD), half),
                pltpu.VMEM((video_count, 2, audio_all, HEAD), half),
                pltpu.VMEM((audio_count, 3, audio_all, HEAD), half),
                pltpu.VMEM((audio_count, audio_all, HEAD), half),
                pltpu.VMEM((audio_count, 2, video_all, HEAD), half),
                pltpu.VMEM((video_count, video_all, HEAD), half),
                pltpu.VMEM((audio_count, audio_all, HEAD), half),
                pltpu.SemaphoreType.DMA((video_count, 3)),
                pltpu.SemaphoreType.DMA((audio_count, 3)),
                pltpu.SemaphoreType.DMA((8,)),
                pltpu.SemaphoreType.DMA((2,)),
            ],
            compiler_params=pltpu.CompilerParams(
                collective_id=0, has_side_effects=True, vmem_limit_bytes=48 * 2**20
            ),
        )(
            by_items(video_qkv, HV),
            video_cross_q,
            by_items(audio_kv_v, HV),
            by_items(audio_qkv, HA),
            audio_cross_q,
            by_items(video_kv_a, HA),
            video_gates.reshape(branches * HV, 1, HEAD),
            audio_gates.reshape(branches * HA, 1, HEAD),
            bias.reshape(branches, 1, audio_all),
        )
    )


def solution(mesh):
    placed = (
        P("groups", "seq", None, None),
        P("groups", "seq", None),
        P("groups", "seq", None, None),
        P("groups", "seq", None, None),
        P("groups", "seq", None),
        P("groups", "seq", None, None),
        P("groups"),
        P("groups"),
        P(),
        P(),
    )
    return jax.shard_map(
        functools.partial(on_device, mesh.shape["seq"]),
        mesh=mesh,
        in_specs=placed,
        out_specs=(P("groups", "seq", None), P("groups", "seq", None)),
        check_vma=False,
    )
```

```python
import functools

import jax
import jax.numpy as jnp
from jax import lax
from jax.experimental import pallas as pl
from jax.experimental.pallas import tpu as pltpu
from jax.sharding import PartitionSpec as P

HV = 32
HA = 16
HEAD = 128
PROMPTS = 4
MESH = pl.DeviceIdType.MESH


def attend(queries, key_rows, value_rows, bias):
    scores = lax.dot_general(
        queries, key_rows, (((1,), (1,)), ((), ())), preferred_element_type=jnp.float32
    ) * (HEAD**-0.5)
    if bias is not None:
        scores = scores + bias
    row_max = jnp.max(scores, axis=1, keepdims=True)
    weights = jnp.exp(scores - row_max)
    total = jnp.sum(weights, axis=1, keepdims=True)
    result = jnp.dot(
        weights.astype(jnp.bfloat16), value_rows, preferred_element_type=jnp.float32
    )
    return (result / total).astype(jnp.bfloat16).astype(jnp.float32)


def block_kernel(
    n,
    video_count,
    cross_count,
    audio_count,
    video_block,
    audio_block,
    video_qkv,
    video_q,
    audio_kv,
    audio_qkv,
    audio_q,
    video_kv,
    video_gates,
    audio_gates,
    bias,
    video_out,
    audio_out,
    video_qkv_in,
    video_q_in,
    audio_kv_in,
    audio_qkv_in,
    audio_q_in,
    video_kv_in,
    video_res,
    cross_res,
    audio_res,
    own_home,
    cross_home,
    video_sems,
    cross_sems,
    audio_sems,
    send_sems,
    back_sems,
):
    me = lax.axis_index("seq")
    group = lax.axis_index("groups")
    video_local = video_out.shape[1]
    audio_local = audio_out.shape[1]

    barrier = pltpu.get_barrier_semaphore()

    def greet(k, carry):
        peer = lax.rem(me + k, n)
        pl.semaphore_signal(barrier, inc=1, device_id=(group, peer), device_id_type=MESH)
        return carry

    lax.fori_loop(1, n, greet, 0)
    pl.semaphore_wait(barrier, n - 1)

    video_rows = pl.ds(pl.multiple_of(me * video_local, video_local), video_local)
    audio_rows = pl.ds(pl.multiple_of(me * audio_local, audio_local), audio_local)

    near = n // 2
    half_first = (me // near) * near
    place_in_half = me - half_first
    half_rows = pl.ds(pl.multiple_of(place_in_half * video_local, video_local), video_local)

    def columns(head):
        return pl.ds(pl.multiple_of(head * HEAD, HEAD), HEAD)

    def video_parts(item, slot):
        branch, head = item // HV, lax.rem(item, HV)
        return (
            (
                video_qkv.at[branch, :, :, columns(head)],
                video_qkv_in.at[slot, :, video_rows],
                video_sems.at[slot],
            ),
        )

    def cross_q_parts(item, slot):
        branch, head = item // HV, lax.rem(item, HV)
        return (
            (
                video_q.at[branch, :, columns(head)],
                video_q_in.at[slot, half_rows],
                cross_sems.at[slot, 0],
            ),
        )

    def cross_kv_parts(item, slot):
        branch, head = item // HV, lax.rem(item, HV)
        return (
            (
                audio_kv.at[branch, :, :, columns(head)],
                audio_kv_in.at[slot, :, audio_rows],
                cross_sems.at[slot, 1],
            ),
        )

    def audio_parts(item, slot):
        branch, head = item // HA, lax.rem(item, HA)
        return (
            (
                audio_qkv.at[branch, :, :, columns(head)],
                audio_qkv_in.at[slot, :, audio_rows],
                audio_sems.at[slot, 0],
            ),
            (
                audio_q.at[branch, :, columns(head)],
                audio_q_in.at[slot, audio_rows],
                audio_sems.at[slot, 1],
            ),
            (
                video_kv.at[branch, :, :, columns(head)],
                video_kv_in.at[slot, :, video_rows],
                audio_sems.at[slot, 2],
            ),
        )

    def send(parts, count, slot, first_sem, first, span, ring):
        def items_of(peer):
            return parts(lax.rem(peer, ring) * count + slot, slot)

        def to_peer(k, carry):
            peer = first + lax.rem(me - first + k, span)
            for place, (source, target, sem) in enumerate(items_of(peer)):
                pltpu.make_async_remote_copy(
                    src_ref=source,
                    dst_ref=target,
                    send_sem=send_sems.at[first_sem + place],
                    recv_sem=sem,
                    device_id=(group, peer),
                    device_id_type=MESH,
                ).start()
            return carry

        lax.fori_loop(1, span, to_peer, 0)
        for source, target, sem in items_of(me):
            pltpu.make_async_copy(source, target, sem).start()

    per_video = cross_count // video_count

    def send_video(slot, carry):
        send(video_parts, video_count, slot, 0, 0, n, n)

        def send_cross(j, inner):
            send(cross_q_parts, cross_count, slot * per_video + j, 1, half_first, near, near)
            send(cross_kv_parts, cross_count, slot * per_video + j, 2, 0, n, near)
            return inner

        lax.fori_loop(0, per_video, send_cross, 0)
        return carry

    def send_audio(slot, carry):
        send(audio_parts, audio_count, slot, 3, 0, n, n)
        return carry

    lax.fori_loop(0, video_count, send_video, 0)
    lax.fori_loop(0, audio_count, send_audio, 0)

    def settle(ref, sem):
        pltpu.make_async_copy(ref, ref, sem).wait()

    def give_back(result, slot, out, branch, head, local, base, first, count, place):
        def to_peer(j, carry):
            peer = base + first + j
            source = result.at[slot, pl.ds(pl.multiple_of((first + j) * local, local), local)]
            target = out.at[branch, :, columns(head)]

            @pl.when(peer == me)
            def _():
                pltpu.make_async_copy(source, target, back_sems.at[place]).start()

            @pl.when(peer != me)
            def _():
                pltpu.make_async_remote_copy(
                    src_ref=source,
                    dst_ref=target,
                    send_sem=send_sems.at[6 + place],
                    recv_sem=back_sems.at[place],
                    device_id=(group, peer),
                    device_id_type=MESH,
                ).start()

            return carry

        lax.fori_loop(0, count, to_peer, 0)

    def video_item(slot, carry):
        item = me * video_count + slot
        branch, head = item // HV, lax.rem(item, HV)
        settle(video_qkv_in.at[slot], video_sems.at[slot])
        block = video_block * video_local

        def rows(i, inner):
            here = pl.ds(pl.multiple_of(i * block, block), block)
            own = attend(
                video_qkv_in[slot, 0, here], video_qkv_in[slot, 1], video_qkv_in[slot, 2], None
            )
            video_res[slot, here] = own.astype(jnp.bfloat16)
            give_back(
                video_res, slot, own_home, branch, head, video_local, 0, i * video_block,
                video_block, 0,
            )
            return inner

        lax.fori_loop(0, n // video_block, rows, 0)

        def cross(j, inner):
            cross_item(slot * per_video + j)
            return inner

        lax.fori_loop(0, per_video, cross, 0)
        return carry

    def cross_item(slot):
        item = place_in_half * cross_count + slot
        branch, head = item // HV, lax.rem(item, HV)
        settle(video_q_in.at[slot], cross_sems.at[slot, 0])
        settle(audio_kv_in.at[slot], cross_sems.at[slot, 1])
        block = video_block * video_local

        def rows(i, inner):
            here = pl.ds(pl.multiple_of(i * block, block), block)
            cross = attend(
                video_q_in[slot, here], audio_kv_in[slot, 0], audio_kv_in[slot, 1], bias[branch]
            )
            cross_res[slot, here] = cross.astype(jnp.bfloat16)
            give_back(
                cross_res, slot, cross_home, branch, head, video_local, half_first,
                i * video_block, video_block, 2,
            )
            return inner

        lax.fori_loop(0, near // video_block, rows, 0)

    def audio_item(slot, carry):
        item = me * audio_count + slot
        branch, head = item // HA, lax.rem(item, HA)
        settle(audio_qkv_in.at[slot], audio_sems.at[slot, 0])
        settle(audio_q_in.at[slot], audio_sems.at[slot, 1])
        settle(video_kv_in.at[slot], audio_sems.at[slot, 2])
        block = audio_block * audio_local

        def rows(i, inner):
            here = pl.ds(pl.multiple_of(i * block, block), block)
            own = attend(
                audio_qkv_in[slot, 0, here],
                audio_qkv_in[slot, 1],
                audio_qkv_in[slot, 2],
                bias[branch],
            )
            cross = attend(
                audio_q_in[slot, here], video_kv_in[slot, 0], video_kv_in[slot, 1], None
            )
            audio_res[slot, here] = (own + audio_gates[item] * cross).astype(jnp.bfloat16)
            give_back(
                audio_res, slot, audio_out, branch, head, audio_local, 0, i * audio_block,
                audio_block, 1,
            )
            return inner

        lax.fori_loop(0, n // audio_block, rows, 0)
        return carry

    lax.fori_loop(0, video_count, video_item, 0)
    lax.fori_loop(0, audio_count, audio_item, 0)

    settle(own_home, back_sems.at[0])
    settle(cross_home, back_sems.at[2])
    width = 512

    def combine(i, carry):
        here = pl.ds(pl.multiple_of(i * width, width), width)
        for branch in range(own_home.shape[0]):
            video_out[branch, :, here] = (
                own_home[branch, :, here].astype(jnp.float32)
                + video_gates[branch, :, here] * cross_home[branch, :, here].astype(jnp.float32)
            ).astype(jnp.bfloat16)
        return carry

    lax.fori_loop(0, video_out.shape[2] // width, combine, 0)

    far_video = pl.ds(0, (n - 1) * video_local)
    far_audio = pl.ds(0, (n - 1) * audio_local)
    far_half = pl.ds(0, (near - 1) * video_local)
    settle(video_qkv_in.at[:, :, far_video], send_sems.at[0])
    settle(video_q_in.at[:, far_half], send_sems.at[1])
    settle(audio_kv_in.at[:, :, far_audio], send_sems.at[2])
    settle(audio_qkv_in.at[:, :, far_audio], send_sems.at[3])
    settle(audio_q_in.at[:, far_audio], send_sems.at[4])
    settle(video_kv_in.at[:, :, far_video], send_sems.at[5])
    settle(video_res.at[:, far_video], send_sems.at[6])
    settle(audio_res.at[:, far_audio], send_sems.at[7])
    settle(cross_res.at[:, far_half], send_sems.at[8])
    settle(audio_out, back_sems.at[1])


def kinds_first(source):
    return jnp.transpose(source, (0, 2, 1, 3))


def on_device(
    n,
    video_qkv,
    video_cross_q,
    audio_kv_v,
    audio_qkv,
    audio_cross_q,
    video_kv_a,
    audio_valid,
    branch_prompt,
    video_gate,
    audio_gate,
):
    branches, video_local = video_cross_q.shape[:2]
    audio_local = audio_cross_q.shape[1]
    video_all, audio_all = video_local * n, audio_local * n
    video_count, audio_count = branches * HV // n, branches * HA // n
    near = n // 2
    cross_count = branches * HV // near
    positions = jnp.arange(audio_all, dtype=jnp.int32)
    bias = jnp.where(positions[None, :] < audio_valid[:, None], 0.0, -jnp.inf).astype(jnp.float32)
    chosen = (branch_prompt[:, None] == jnp.arange(PROMPTS, dtype=jnp.int32)[None, :]).astype(
        jnp.float32
    )
    video_gates = jnp.dot(chosen, video_gate, precision=lax.Precision.HIGHEST)
    audio_gates = jnp.dot(chosen, audio_gate, precision=lax.Precision.HIGHEST)
    hbm = pl.BlockSpec(memory_space=pl.ANY)
    vmem = pl.BlockSpec(memory_space=pltpu.VMEM)
    half = jnp.bfloat16
    return tuple(
        pl.pallas_call(
            functools.partial(
                block_kernel, n, video_count, cross_count, audio_count, min(4, near), min(8, n)
            ),
            out_shape=(
                jax.ShapeDtypeStruct(video_cross_q.shape, half),
                jax.ShapeDtypeStruct(audio_cross_q.shape, half),
            ),
            in_specs=[hbm] * 6 + [vmem] * 3,
            out_specs=(vmem, hbm),
            scratch_shapes=[
                pltpu.VMEM((video_count, 3, video_all, HEAD), half),
                pltpu.VMEM((cross_count, near * video_local, HEAD), half),
                pltpu.VMEM((cross_count, 2, audio_all, HEAD), half),
                pltpu.VMEM((audio_count, 3, audio_all, HEAD), half),
                pltpu.VMEM((audio_count, audio_all, HEAD), half),
                pltpu.VMEM((audio_count, 2, video_all, HEAD), half),
                pltpu.VMEM((video_count, video_all, HEAD), half),
                pltpu.VMEM((cross_count, near * video_local, HEAD), half),
                pltpu.VMEM((audio_count, audio_all, HEAD), half),
                pltpu.VMEM(video_cross_q.shape, half),
                pltpu.VMEM(video_cross_q.shape, half),
                pltpu.SemaphoreType.DMA((video_count,)),
                pltpu.SemaphoreType.DMA((cross_count, 2)),
                pltpu.SemaphoreType.DMA((audio_count, 3)),
                pltpu.SemaphoreType.DMA((9,)),
                pltpu.SemaphoreType.DMA((3,)),
            ],
            compiler_params=pltpu.CompilerParams(
                collective_id=0, has_side_effects=True, vmem_limit_bytes=52 * 2**20
            ),
        )(
            kinds_first(video_qkv),
            video_cross_q,
            kinds_first(audio_kv_v),
            kinds_first(audio_qkv),
            audio_cross_q,
            kinds_first(video_kv_a),
            video_gates.reshape(branches, 1, -1),
            audio_gates.reshape(branches * HA, 1, HEAD),
            bias.reshape(branches, 1, audio_all),
        )
    )


def solution(mesh):
    placed = (
        P("groups", "seq", None, None),
        P("groups", "seq", None),
        P("groups", "seq", None, None),
        P("groups", "seq", None, None),
        P("groups", "seq", None),
        P("groups", "seq", None, None),
        P("groups"),
        P("groups"),
        P(),
        P(),
    )
    return jax.shard_map(
        functools.partial(on_device, mesh.shape["seq"]),
        mesh=mesh,
        in_specs=placed,
        out_specs=(P("groups", "seq", None), P("groups", "seq", None)),
        check_vma=False,
    )
```

```python
import functools

import jax
import jax.numpy as jnp
from jax import lax
from jax.experimental import pallas as pl
from jax.experimental.pallas import tpu as pltpu
from jax.sharding import PartitionSpec as P

HV = 32
HA = 16
HEAD = 128
PROMPTS = 4
MESH = pl.DeviceIdType.MESH


def attend(queries, key_rows, value_rows, bias):
    scores = lax.dot_general(
        queries, key_rows, (((1,), (1,)), ((), ())), preferred_element_type=jnp.float32
    ) * (HEAD**-0.5)
    if bias is not None:
        scores = scores + bias
    row_max = jnp.max(scores, axis=1, keepdims=True)
    weights = jnp.exp(scores - row_max)
    total = jnp.sum(weights, axis=1, keepdims=True)
    result = jnp.dot(
        weights.astype(jnp.bfloat16), value_rows, preferred_element_type=jnp.float32
    )
    return result / total, row_max + jnp.log(total)


def block_kernel(
    n,
    video_count,
    cross_count,
    audio_count,
    across_count,
    video_block,
    audio_block,
    video_qkv,
    video_q,
    audio_kv,
    audio_qkv,
    audio_q,
    video_kv,
    video_gates,
    audio_gates,
    bias,
    video_out,
    audio_out,
    video_qkv_in,
    video_q_in,
    audio_kv_in,
    audio_qkv_in,
    audio_q_in,
    video_kv_in,
    video_res,
    cross_res,
    audio_res,
    across_res,
    level_res,
    own_home,
    cross_home,
    audio_home,
    across_home,
    level_home,
    share_mat,
    video_sems,
    cross_sems,
    audio_sems,
    across_sems,
    send_sems,
    back_sems,
):
    me = lax.axis_index("seq")
    group = lax.axis_index("groups")
    video_local = video_out.shape[1]
    audio_local = audio_out.shape[1]

    barrier = pltpu.get_barrier_semaphore()

    def greet(k, carry):
        peer = lax.rem(me + k, n)
        pl.semaphore_signal(barrier, inc=1, device_id=(group, peer), device_id_type=MESH)
        return carry

    lax.fori_loop(1, n, greet, 0)
    pl.semaphore_wait(barrier, n - 1)

    video_rows = pl.ds(pl.multiple_of(me * video_local, video_local), video_local)
    audio_rows = pl.ds(pl.multiple_of(me * audio_local, audio_local), audio_local)

    near = n // 2
    half_first = (me // near) * near
    place_in_half = me - half_first
    half_rows = pl.ds(pl.multiple_of(place_in_half * video_local, video_local), video_local)

    def columns(head):
        return pl.ds(pl.multiple_of(head * HEAD, HEAD), HEAD)

    def video_parts(item, slot):
        branch, head = item // HV, lax.rem(item, HV)
        return (
            (
                video_qkv.at[branch, :, :, columns(head)],
                video_qkv_in.at[slot, :, video_rows],
                video_sems.at[slot],
            ),
        )

    def cross_q_parts(item, slot):
        branch, head = item // HV, lax.rem(item, HV)
        return (
            (
                video_q.at[branch, :, columns(head)],
                video_q_in.at[slot, half_rows],
                cross_sems.at[slot, 0],
            ),
        )

    def cross_kv_parts(item, slot):
        branch, head = item // HV, lax.rem(item, HV)
        return (
            (
                audio_kv.at[branch, :, :, columns(head)],
                audio_kv_in.at[slot, :, audio_rows],
                cross_sems.at[slot, 1],
            ),
        )

    def audio_parts(item, slot):
        branch, head = item // HA, lax.rem(item, HA)
        return (
            (
                audio_qkv.at[branch, :, :, columns(head)],
                audio_qkv_in.at[slot, :, audio_rows],
                audio_sems.at[slot],
            ),
        )

    def across_q_parts(item, slot):
        branch, head = item // HA, lax.rem(item, HA)
        return (
            (
                audio_q.at[branch, :, columns(head)],
                audio_q_in.at[slot, audio_rows],
                across_sems.at[slot, 0],
            ),
        )

    def across_kv_parts(item, slot):
        branch, head = item // HA, lax.rem(item, HA)
        return (
            (
                video_kv.at[branch, :, :, columns(head)],
                video_kv_in.at[slot, :, half_rows],
                across_sems.at[slot, 1],
            ),
        )

    def send(parts, count, slot, first_sem, first, span, ring):
        def items_of(peer):
            return parts(lax.rem(peer, ring) * count + slot, slot)

        def to_peer(k, carry):
            peer = first + lax.rem(me - first + k, span)
            for place, (source, target, sem) in enumerate(items_of(peer)):
                pltpu.make_async_remote_copy(
                    src_ref=source,
                    dst_ref=target,
                    send_sem=send_sems.at[first_sem + place],
                    recv_sem=sem,
                    device_id=(group, peer),
                    device_id_type=MESH,
                ).start()
            return carry

        lax.fori_loop(1, span, to_peer, 0)
        for source, target, sem in items_of(me):
            pltpu.make_async_copy(source, target, sem).start()

    per_video = cross_count // video_count
    per_audio = across_count // audio_count

    def send_video(slot, carry):
        send(video_parts, video_count, slot, 0, 0, n, n)

        def send_cross(j, inner):
            send(cross_q_parts, cross_count, slot * per_video + j, 1, half_first, near, near)
            send(cross_kv_parts, cross_count, slot * per_video + j, 2, 0, n, near)
            return inner

        lax.fori_loop(0, per_video, send_cross, 0)
        return carry

    def send_audio(slot, carry):
        send(audio_parts, audio_count, slot, 3, 0, n, n)

        def send_across(j, inner):
            send(across_q_parts, across_count, slot * per_audio + j, 4, 0, n, near)
            send(across_kv_parts, across_count, slot * per_audio + j, 5, half_first, near, near)
            return inner

        lax.fori_loop(0, per_audio, send_across, 0)
        return carry

    lax.fori_loop(0, video_count, send_video, 0)
    lax.fori_loop(0, audio_count, send_audio, 0)

    def settle(ref, sem):
        pltpu.make_async_copy(ref, ref, sem).wait()

    def give_back(result, slot, out, branch, head, local, base, first, count, place):
        def to_peer(j, carry):
            peer = base + first + j
            source = result.at[slot, pl.ds(pl.multiple_of((first + j) * local, local), local)]
            target = out.at[branch, :, columns(head)]

            @pl.when(peer == me)
            def _():
                pltpu.make_async_copy(source, target, back_sems.at[place]).start()

            @pl.when(peer != me)
            def _():
                pltpu.make_async_remote_copy(
                    src_ref=source,
                    dst_ref=target,
                    send_sem=send_sems.at[6 + place],
                    recv_sem=back_sems.at[place],
                    device_id=(group, peer),
                    device_id_type=MESH,
                ).start()

            return carry

        lax.fori_loop(0, count, to_peer, 0)

    def video_item(slot, carry):
        item = me * video_count + slot
        branch, head = item // HV, lax.rem(item, HV)
        settle(video_qkv_in.at[slot], video_sems.at[slot])
        block = video_block * video_local

        def rows(i, inner):
            here = pl.ds(pl.multiple_of(i * block, block), block)
            own, _ = attend(
                video_qkv_in[slot, 0, here], video_qkv_in[slot, 1], video_qkv_in[slot, 2], None
            )
            video_res[slot, here] = own.astype(jnp.bfloat16)
            give_back(
                video_res, slot, own_home, branch, head, video_local, 0, i * video_block,
                video_block, 0,
            )
            return inner

        lax.fori_loop(0, n // video_block, rows, 0)

        def cross(j, inner):
            cross_item(slot * per_video + j)
            return inner

        lax.fori_loop(0, per_video, cross, 0)
        return carry

    def cross_item(slot):
        item = place_in_half * cross_count + slot
        branch, head = item // HV, lax.rem(item, HV)
        settle(video_q_in.at[slot], cross_sems.at[slot, 0])
        settle(audio_kv_in.at[slot], cross_sems.at[slot, 1])
        block = video_block * video_local

        def rows(i, inner):
            here = pl.ds(pl.multiple_of(i * block, block), block)
            cross, _ = attend(
                video_q_in[slot, here], audio_kv_in[slot, 0], audio_kv_in[slot, 1], bias[branch]
            )
            cross_res[slot, here] = cross.astype(jnp.bfloat16)
            give_back(
                cross_res, slot, cross_home, branch, head, video_local, half_first,
                i * video_block, video_block, 2,
            )
            return inner

        lax.fori_loop(0, near // video_block, rows, 0)

    def audio_item(slot, carry):
        item = me * audio_count + slot
        branch, head = item // HA, lax.rem(item, HA)
        settle(audio_qkv_in.at[slot], audio_sems.at[slot])
        block = audio_block * audio_local

        def rows(i, inner):
            here = pl.ds(pl.multiple_of(i * block, block), block)
            own, _ = attend(
                audio_qkv_in[slot, 0, here],
                audio_qkv_in[slot, 1],
                audio_qkv_in[slot, 2],
                bias[branch],
            )
            audio_res[slot, here] = own.astype(jnp.bfloat16)
            give_back(
                audio_res, slot, audio_home, branch, head, audio_local, 0, i * audio_block,
                audio_block, 1,
            )
            return inner

        lax.fori_loop(0, n // audio_block, rows, 0)

        def across(j, inner):
            across_item(slot * per_audio + j)
            return inner

        lax.fori_loop(0, per_audio, across, 0)
        return carry

    my_half = me // near

    def across_item(slot):
        item = place_in_half * across_count + slot
        branch, head = item // HA, lax.rem(item, HA)
        settle(audio_q_in.at[slot], across_sems.at[slot, 0])
        settle(video_kv_in.at[slot], across_sems.at[slot, 1])
        block = audio_block * audio_local

        def rows(i, inner):
            here = pl.ds(pl.multiple_of(i * block, block), block)
            part, level = attend(
                audio_q_in[slot, here], video_kv_in[slot, 0], video_kv_in[slot, 1], None
            )
            across_res[slot, here] = part.astype(jnp.bfloat16)
            for c in range(block // HEAD):
                column = jnp.broadcast_to(level[c * HEAD : (c + 1) * HEAD], (HEAD, HEAD))
                level_res[slot, i * (block // HEAD) + c] = jnp.transpose(column)[0:1]
            give_back(
                across_res, slot, across_home.at[my_half], branch, head, audio_local, 0,
                i * audio_block, audio_block, 3,
            )
            return inner

        lax.fori_loop(0, n // audio_block, rows, 0)

        def levels(k, inner):
            peer = lax.rem(me + k, n)
            pltpu.make_async_remote_copy(
                src_ref=level_res.at[slot, (peer * audio_local) // HEAD],
                dst_ref=level_home.at[my_half * (audio_home.shape[0] * HA) + item],
                send_sem=send_sems.at[10],
                recv_sem=back_sems.at[4],
                device_id=(group, peer),
                device_id_type=MESH,
            ).start()
            return inner

        lax.fori_loop(1, n, levels, 0)
        pltpu.make_async_copy(
            level_res.at[slot, (me * audio_local) // HEAD],
            level_home.at[my_half * (audio_home.shape[0] * HA) + item],
            back_sems.at[4],
        ).start()

    lax.fori_loop(0, video_count, video_item, 0)
    lax.fori_loop(0, audio_count, audio_item, 0)

    settle(own_home, back_sems.at[0])
    settle(cross_home, back_sems.at[2])
    width = 512

    def combine(i, carry):
        here = pl.ds(pl.multiple_of(i * width, width), width)
        for branch in range(own_home.shape[0]):
            video_out[branch, :, here] = (
                own_home[branch, :, here].astype(jnp.float32)
                + video_gates[branch, :, here] * cross_home[branch, :, here].astype(jnp.float32)
            ).astype(jnp.bfloat16)
        return carry

    lax.fori_loop(0, video_out.shape[2] // width, combine, 0)

    settle(audio_home, back_sems.at[1])
    settle(across_home, back_sems.at[3])
    settle(level_home, back_sems.at[4])
    items = level_home.shape[0] // 2
    low, high = level_home[:items, 0], level_home[items:, 0]
    for place, gap in enumerate((high - low, low - high)):
        share_mat[place] = jnp.transpose(1.0 / (1.0 + jnp.exp(gap)))
    mine = pl.ds(pl.multiple_of(lax.rem(me * audio_local, HEAD), audio_local), audio_local)
    low_share, high_share = share_mat[0, mine], share_mat[1, mine]
    for item in range(low_share.shape[1]):
        branch, head = item // HA, item % HA
        here = slice(head * HEAD, (head + 1) * HEAD)
        across = (
            low_share[:, item : item + 1] * across_home[0, branch, :, here].astype(jnp.float32)
            + high_share[:, item : item + 1] * across_home[1, branch, :, here].astype(jnp.float32)
        )
        audio_out[branch, :, here] = (
            audio_home[branch, :, here].astype(jnp.float32) + audio_gates[item] * across
        ).astype(jnp.bfloat16)

    far_video = pl.ds(0, (n - 1) * video_local)
    far_audio = pl.ds(0, (n - 1) * audio_local)
    far_half = pl.ds(0, (near - 1) * video_local)
    settle(video_qkv_in.at[:, :, far_video], send_sems.at[0])
    settle(video_q_in.at[:, far_half], send_sems.at[1])
    settle(audio_kv_in.at[:, :, far_audio], send_sems.at[2])
    settle(audio_qkv_in.at[:, :, far_audio], send_sems.at[3])
    settle(audio_q_in.at[:, far_audio], send_sems.at[4])
    settle(video_kv_in.at[:, :, far_half], send_sems.at[5])
    settle(video_res.at[:, far_video], send_sems.at[6])
    settle(audio_res.at[:, far_audio], send_sems.at[7])
    settle(cross_res.at[:, far_half], send_sems.at[8])
    settle(across_res.at[:, far_audio], send_sems.at[9])
    settle(level_home.at[pl.ds(0, across_count * (n - 1))], send_sems.at[10])


def kinds_first(source):
    return jnp.transpose(source, (0, 2, 1, 3))


def on_device(
    n,
    video_qkv,
    video_cross_q,
    audio_kv_v,
    audio_qkv,
    audio_cross_q,
    video_kv_a,
    audio_valid,
    branch_prompt,
    video_gate,
    audio_gate,
):
    branches, video_local = video_cross_q.shape[:2]
    audio_local = audio_cross_q.shape[1]
    video_all, audio_all = video_local * n, audio_local * n
    video_count, audio_count = branches * HV // n, branches * HA // n
    near = n // 2
    cross_count, across_count = branches * HV // near, branches * HA // near
    positions = jnp.arange(audio_all, dtype=jnp.int32)
    bias = jnp.where(positions[None, :] < audio_valid[:, None], 0.0, -jnp.inf).astype(jnp.float32)
    chosen = (branch_prompt[:, None] == jnp.arange(PROMPTS, dtype=jnp.int32)[None, :]).astype(
        jnp.float32
    )
    video_gates = jnp.dot(chosen, video_gate, precision=lax.Precision.HIGHEST)
    audio_gates = jnp.dot(chosen, audio_gate, precision=lax.Precision.HIGHEST)
    hbm = pl.BlockSpec(memory_space=pl.ANY)
    vmem = pl.BlockSpec(memory_space=pltpu.VMEM)
    half = jnp.bfloat16
    return tuple(
        pl.pallas_call(
            functools.partial(
                block_kernel, n, video_count, cross_count, audio_count, across_count, min(4, near), min(8, n)
            ),
            out_shape=(
                jax.ShapeDtypeStruct(video_cross_q.shape, half),
                jax.ShapeDtypeStruct(audio_cross_q.shape, half),
            ),
            in_specs=[hbm] * 6 + [vmem] * 3,
            out_specs=(vmem, vmem),
            scratch_shapes=[
                pltpu.VMEM((video_count, 3, video_all, HEAD), half),
                pltpu.VMEM((cross_count, near * video_local, HEAD), half),
                pltpu.VMEM((cross_count, 2, audio_all, HEAD), half),
                pltpu.VMEM((audio_count, 3, audio_all, HEAD), half),
                pltpu.VMEM((across_count, audio_all, HEAD), half),
                pltpu.VMEM((across_count, 2, near * video_local, HEAD), half),
                pltpu.VMEM((video_count, video_all, HEAD), half),
                pltpu.VMEM((cross_count, near * video_local, HEAD), half),
                pltpu.VMEM((audio_count, audio_all, HEAD), half),
                pltpu.VMEM((across_count, audio_all, HEAD), half),
                pltpu.VMEM((across_count, audio_all // HEAD, 1, HEAD), jnp.float32),
                pltpu.VMEM(video_cross_q.shape, half),
                pltpu.VMEM(video_cross_q.shape, half),
                pltpu.VMEM(audio_cross_q.shape, half),
                pltpu.VMEM((2,) + audio_cross_q.shape, half),
                pltpu.VMEM((2 * branches * HA, 1, HEAD), jnp.float32),
                pltpu.VMEM((2, HEAD, branches * HA), jnp.float32),
                pltpu.SemaphoreType.DMA((video_count,)),
                pltpu.SemaphoreType.DMA((cross_count, 2)),
                pltpu.SemaphoreType.DMA((audio_count,)),
                pltpu.SemaphoreType.DMA((across_count, 2)),
                pltpu.SemaphoreType.DMA((11,)),
                pltpu.SemaphoreType.DMA((5,)),
            ],
            compiler_params=pltpu.CompilerParams(
                collective_id=0, has_side_effects=True, vmem_limit_bytes=52 * 2**20
            ),
        )(
            kinds_first(video_qkv),
            video_cross_q,
            kinds_first(audio_kv_v),
            kinds_first(audio_qkv),
            audio_cross_q,
            kinds_first(video_kv_a),
            video_gates.reshape(branches, 1, -1),
            audio_gates.reshape(branches * HA, 1, HEAD),
            bias.reshape(branches, 1, audio_all),
        )
    )


def solution(mesh):
    placed = (
        P("groups", "seq", None, None),
        P("groups", "seq", None),
        P("groups", "seq", None, None),
        P("groups", "seq", None, None),
        P("groups", "seq", None),
        P("groups", "seq", None, None),
        P("groups"),
        P("groups"),
        P(),
        P(),
    )
    return jax.shard_map(
        functools.partial(on_device, mesh.shape["seq"]),
        mesh=mesh,
        in_specs=placed,
        out_specs=(P("groups", "seq", None), P("groups", "seq", None)),
        check_vma=False,
    )
```

```python
import functools

import jax
import jax.numpy as jnp
from jax import lax
from jax.experimental import pallas as pl
from jax.experimental.pallas import tpu as pltpu
from jax.sharding import PartitionSpec as P

HV = 32
HA = 16
HEAD = 128
PROMPTS = 4
MESH = pl.DeviceIdType.MESH


def attend(queries, key_rows, value_rows, bias):
    scores = lax.dot_general(
        queries, key_rows, (((1,), (1,)), ((), ())), preferred_element_type=jnp.float32
    ) * (HEAD**-0.5)
    if bias is not None:
        scores = scores + bias
    row_max = jnp.max(scores, axis=1, keepdims=True)
    weights = jnp.exp(scores - row_max)
    total = jnp.sum(weights, axis=1, keepdims=True)
    result = jnp.dot(
        weights.astype(jnp.bfloat16), value_rows, preferred_element_type=jnp.float32
    )
    return result / total, row_max + jnp.log(total)


def block_kernel(
    n,
    video_count,
    cross_count,
    audio_count,
    across_count,
    video_block,
    audio_block,
    video_qkv,
    video_q,
    audio_kv,
    audio_qkv,
    audio_q,
    video_kv,
    video_gates,
    audio_gates,
    bias,
    video_out,
    audio_out,
    video_qkv_in,
    video_q_in,
    audio_kv_in,
    audio_qkv_in,
    audio_q_in,
    video_kv_in,
    video_res,
    cross_res,
    audio_res,
    across_res,
    level_res,
    own_home,
    cross_home,
    audio_home,
    across_home,
    level_home,
    share_mat,
    video_sems,
    cross_sems,
    audio_sems,
    across_sems,
    send_sems,
    back_sems,
):
    me = lax.axis_index("seq")
    group = lax.axis_index("groups")
    video_local = video_out.shape[1]
    audio_local = audio_out.shape[1]

    barrier = pltpu.get_barrier_semaphore()

    def greet(k, carry):
        peer = lax.rem(me + k, n)
        pl.semaphore_signal(barrier, inc=1, device_id=(group, peer), device_id_type=MESH)
        return carry

    lax.fori_loop(1, n, greet, 0)
    pl.semaphore_wait(barrier, n - 1)

    video_rows = pl.ds(pl.multiple_of(me * video_local, video_local), video_local)
    audio_rows = pl.ds(pl.multiple_of(me * audio_local, audio_local), audio_local)

    near = n // 2
    half_first = (me // near) * near
    place_in_half = me - half_first
    half_rows = pl.ds(pl.multiple_of(place_in_half * video_local, video_local), video_local)

    def columns(head):
        return pl.ds(pl.multiple_of(head * HEAD, HEAD), HEAD)

    def video_parts(item, slot):
        branch, head = item // HV, lax.rem(item, HV)
        return (
            (
                video_qkv.at[branch, :, :, columns(head)],
                video_qkv_in.at[slot, :, video_rows],
                video_sems.at[slot],
            ),
        )

    def cross_q_parts(item, slot):
        branch, head = item // HV, lax.rem(item, HV)
        return (
            (
                video_q.at[branch, :, columns(head)],
                video_q_in.at[slot, half_rows],
                cross_sems.at[slot, 0],
            ),
        )

    def cross_kv_parts(item, slot):
        branch, head = item // HV, lax.rem(item, HV)
        return (
            (
                audio_kv.at[branch, :, :, columns(head)],
                audio_kv_in.at[slot, :, audio_rows],
                cross_sems.at[slot, 1],
            ),
        )

    def audio_parts(item, slot):
        branch, head = item // HA, lax.rem(item, HA)
        return (
            (
                audio_qkv.at[branch, :, :, columns(head)],
                audio_qkv_in.at[slot, :, audio_rows],
                audio_sems.at[slot],
            ),
        )

    def across_q_parts(item, slot):
        branch, head = item // HA, lax.rem(item, HA)
        return (
            (
                audio_q.at[branch, :, columns(head)],
                audio_q_in.at[slot, audio_rows],
                across_sems.at[slot, 0],
            ),
        )

    def across_kv_parts(item, slot):
        branch, head = item // HA, lax.rem(item, HA)
        return (
            (
                video_kv.at[branch, :, :, columns(head)],
                video_kv_in.at[slot, :, half_rows],
                across_sems.at[slot, 1],
            ),
        )

    def send(parts, count, slot, first_sem, first, span, ring):
        def items_of(peer):
            return parts(lax.rem(peer, ring) * count + slot, slot)

        def to_peer(k, carry):
            peer = first + lax.rem(me - first + k, span)
            for place, (source, target, sem) in enumerate(items_of(peer)):
                pltpu.make_async_remote_copy(
                    src_ref=source,
                    dst_ref=target,
                    send_sem=send_sems.at[first_sem + place],
                    recv_sem=sem,
                    device_id=(group, peer),
                    device_id_type=MESH,
                ).start()
            return carry

        lax.fori_loop(1, span, to_peer, 0)
        for source, target, sem in items_of(me):
            pltpu.make_async_copy(source, target, sem).start()

    per_video = cross_count // (video_count - audio_count)
    per_audio = across_count // audio_count

    def send_video(slot, carry):
        send(video_parts, video_count, slot, 0, 0, n, n)
        return carry

    def send_crosses(slot, carry):
        first = (slot - audio_count) * per_video

        def send_cross(j, inner):
            send(cross_kv_parts, cross_count, first + j, 2, 0, n, near)
            send(cross_q_parts, cross_count, first + j, 1, half_first, near, near)
            return inner

        lax.fori_loop(0, per_video, send_cross, 0)
        return carry

    def send_audio(slot, carry):
        send(audio_parts, audio_count, slot, 3, 0, n, n)

        def send_across(j, inner):
            send(across_q_parts, across_count, slot * per_audio + j, 4, 0, n, near)
            send(across_kv_parts, across_count, slot * per_audio + j, 5, half_first, near, near)
            return inner

        lax.fori_loop(0, per_audio, send_across, 0)
        return carry

    def early(slot, carry, video, other):
        video(slot, carry)
        return other(slot, carry)

    lax.fori_loop(
        0, audio_count, functools.partial(early, video=send_video, other=send_audio), 0
    )
    lax.fori_loop(
        audio_count,
        video_count,
        functools.partial(early, video=send_video, other=send_crosses),
        0,
    )

    def settle(ref, sem):
        pltpu.make_async_copy(ref, ref, sem).wait()

    def give_back(result, slot, out, branch, head, local, base, first, count, place):
        def to_peer(j, carry):
            peer = base + first + j
            source = result.at[slot, pl.ds(pl.multiple_of((first + j) * local, local), local)]
            target = out.at[branch, :, columns(head)]

            @pl.when(peer == me)
            def _():
                pltpu.make_async_copy(source, target, back_sems.at[place]).start()

            @pl.when(peer != me)
            def _():
                pltpu.make_async_remote_copy(
                    src_ref=source,
                    dst_ref=target,
                    send_sem=send_sems.at[6 + place],
                    recv_sem=back_sems.at[place],
                    device_id=(group, peer),
                    device_id_type=MESH,
                ).start()

            return carry

        lax.fori_loop(0, count, to_peer, 0)

    def video_item(slot, carry):
        item = me * video_count + slot
        branch, head = item // HV, lax.rem(item, HV)
        settle(video_qkv_in.at[slot], video_sems.at[slot])
        block = video_block * video_local

        def rows(i, inner):
            here = pl.ds(pl.multiple_of(i * block, block), block)
            own, _ = attend(
                video_qkv_in[slot, 0, here], video_qkv_in[slot, 1], video_qkv_in[slot, 2], None
            )
            video_res[slot, here] = own.astype(jnp.bfloat16)
            give_back(
                video_res, slot, own_home, branch, head, video_local, 0, i * video_block,
                video_block, 0,
            )
            return inner

        lax.fori_loop(0, n // video_block, rows, 0)
        return carry

    def cross_items(slot, carry):
        def cross(j, inner):
            cross_item((slot - audio_count) * per_video + j)
            return inner

        lax.fori_loop(0, per_video, cross, 0)
        return carry

    def cross_item(slot):
        item = place_in_half * cross_count + slot
        branch, head = item // HV, lax.rem(item, HV)
        settle(video_q_in.at[slot], cross_sems.at[slot, 0])
        settle(audio_kv_in.at[slot], cross_sems.at[slot, 1])
        block = video_block * video_local

        def rows(i, inner):
            here = pl.ds(pl.multiple_of(i * block, block), block)
            cross, _ = attend(
                video_q_in[slot, here], audio_kv_in[slot, 0], audio_kv_in[slot, 1], bias[branch]
            )
            cross_res[slot, here] = cross.astype(jnp.bfloat16)
            give_back(
                cross_res, slot, cross_home, branch, head, video_local, half_first,
                i * video_block, video_block, 2,
            )
            return inner

        lax.fori_loop(0, near // video_block, rows, 0)

    def audio_item(slot, carry):
        item = me * audio_count + slot
        branch, head = item // HA, lax.rem(item, HA)
        settle(audio_qkv_in.at[slot], audio_sems.at[slot])
        block = audio_block * audio_local

        def rows(i, inner):
            here = pl.ds(pl.multiple_of(i * block, block), block)
            own, _ = attend(
                audio_qkv_in[slot, 0, here],
                audio_qkv_in[slot, 1],
                audio_qkv_in[slot, 2],
                bias[branch],
            )
            audio_res[slot, here] = own.astype(jnp.bfloat16)
            give_back(
                audio_res, slot, audio_home, branch, head, audio_local, 0, i * audio_block,
                audio_block, 1,
            )
            return inner

        lax.fori_loop(0, n // audio_block, rows, 0)

        def across(j, inner):
            across_item(slot * per_audio + j)
            return inner

        lax.fori_loop(0, per_audio, across, 0)
        return carry

    my_half = me // near

    def across_item(slot):
        item = place_in_half * across_count + slot
        branch, head = item // HA, lax.rem(item, HA)
        settle(audio_q_in.at[slot], across_sems.at[slot, 0])
        settle(video_kv_in.at[slot], across_sems.at[slot, 1])
        block = audio_block * audio_local

        def rows(i, inner):
            here = pl.ds(pl.multiple_of(i * block, block), block)
            part, level = attend(
                audio_q_in[slot, here], video_kv_in[slot, 0], video_kv_in[slot, 1], None
            )
            across_res[slot, here] = part.astype(jnp.bfloat16)
            for c in range(block // HEAD):
                column = jnp.broadcast_to(level[c * HEAD : (c + 1) * HEAD], (HEAD, HEAD))
                level_res[slot, i * (block // HEAD) + c] = jnp.transpose(column)[0:1]
            give_back(
                across_res, slot, across_home.at[my_half], branch, head, audio_local, 0,
                i * audio_block, audio_block, 3,
            )
            return inner

        lax.fori_loop(0, n // audio_block, rows, 0)

        def levels(k, inner):
            peer = lax.rem(me + k, n)
            pltpu.make_async_remote_copy(
                src_ref=level_res.at[slot, (peer * audio_local) // HEAD],
                dst_ref=level_home.at[my_half * (audio_home.shape[0] * HA) + item],
                send_sem=send_sems.at[10],
                recv_sem=back_sems.at[4],
                device_id=(group, peer),
                device_id_type=MESH,
            ).start()
            return inner

        lax.fori_loop(1, n, levels, 0)
        pltpu.make_async_copy(
            level_res.at[slot, (me * audio_local) // HEAD],
            level_home.at[my_half * (audio_home.shape[0] * HA) + item],
            back_sems.at[4],
        ).start()

    lax.fori_loop(
        0, audio_count, functools.partial(early, video=video_item, other=audio_item), 0
    )
    lax.fori_loop(
        audio_count,
        video_count,
        functools.partial(early, video=video_item, other=cross_items),
        0,
    )

    settle(audio_home, back_sems.at[1])
    settle(across_home, back_sems.at[3])
    settle(level_home, back_sems.at[4])
    items = level_home.shape[0] // 2
    low, high = level_home[:items, 0], level_home[items:, 0]
    for place, gap in enumerate((high - low, low - high)):
        share_mat[place] = jnp.transpose(1.0 / (1.0 + jnp.exp(gap)))
    mine = pl.ds(pl.multiple_of(lax.rem(me * audio_local, HEAD), audio_local), audio_local)
    low_share, high_share = share_mat[0, mine], share_mat[1, mine]
    for item in range(low_share.shape[1]):
        branch, head = item // HA, item % HA
        here = slice(head * HEAD, (head + 1) * HEAD)
        across = (
            low_share[:, item : item + 1] * across_home[0, branch, :, here].astype(jnp.float32)
            + high_share[:, item : item + 1] * across_home[1, branch, :, here].astype(jnp.float32)
        )
        audio_out[branch, :, here] = (
            audio_home[branch, :, here].astype(jnp.float32) + audio_gates[item] * across
        ).astype(jnp.bfloat16)

    settle(own_home, back_sems.at[0])
    settle(cross_home, back_sems.at[2])
    width = 512

    def combine(i, carry):
        here = pl.ds(pl.multiple_of(i * width, width), width)
        for branch in range(own_home.shape[0]):
            video_out[branch, :, here] = (
                own_home[branch, :, here].astype(jnp.float32)
                + video_gates[branch, :, here] * cross_home[branch, :, here].astype(jnp.float32)
            ).astype(jnp.bfloat16)
        return carry

    lax.fori_loop(0, video_out.shape[2] // width, combine, 0)

    far_video = pl.ds(0, (n - 1) * video_local)
    far_audio = pl.ds(0, (n - 1) * audio_local)
    far_half = pl.ds(0, (near - 1) * video_local)
    settle(video_qkv_in.at[:, :, far_video], send_sems.at[0])
    settle(video_q_in.at[:, far_half], send_sems.at[1])
    settle(audio_kv_in.at[:, :, far_audio], send_sems.at[2])
    settle(audio_qkv_in.at[:, :, far_audio], send_sems.at[3])
    settle(audio_q_in.at[:, far_audio], send_sems.at[4])
    settle(video_kv_in.at[:, :, far_half], send_sems.at[5])
    settle(video_res.at[:, far_video], send_sems.at[6])
    settle(audio_res.at[:, far_audio], send_sems.at[7])
    settle(cross_res.at[:, far_half], send_sems.at[8])
    settle(across_res.at[:, far_audio], send_sems.at[9])
    settle(level_home.at[pl.ds(0, across_count * (n - 1))], send_sems.at[10])


def kinds_first(source):
    return jnp.transpose(source, (0, 2, 1, 3))


def on_device(
    n,
    video_qkv,
    video_cross_q,
    audio_kv_v,
    audio_qkv,
    audio_cross_q,
    video_kv_a,
    audio_valid,
    branch_prompt,
    video_gate,
    audio_gate,
):
    branches, video_local = video_cross_q.shape[:2]
    audio_local = audio_cross_q.shape[1]
    video_all, audio_all = video_local * n, audio_local * n
    video_count, audio_count = branches * HV // n, branches * HA // n
    near = n // 2
    cross_count, across_count = branches * HV // near, branches * HA // near
    positions = jnp.arange(audio_all, dtype=jnp.int32)
    bias = jnp.where(positions[None, :] < audio_valid[:, None], 0.0, -jnp.inf).astype(jnp.float32)
    chosen = (branch_prompt[:, None] == jnp.arange(PROMPTS, dtype=jnp.int32)[None, :]).astype(
        jnp.float32
    )
    video_gates = jnp.dot(chosen, video_gate, precision=lax.Precision.HIGHEST)
    audio_gates = jnp.dot(chosen, audio_gate, precision=lax.Precision.HIGHEST)
    hbm = pl.BlockSpec(memory_space=pl.ANY)
    vmem = pl.BlockSpec(memory_space=pltpu.VMEM)
    half = jnp.bfloat16
    return tuple(
        pl.pallas_call(
            functools.partial(
                block_kernel, n, video_count, cross_count, audio_count, across_count, min(4, near), min(8, n)
            ),
            out_shape=(
                jax.ShapeDtypeStruct(video_cross_q.shape, half),
                jax.ShapeDtypeStruct(audio_cross_q.shape, half),
            ),
            in_specs=[hbm] * 6 + [vmem] * 3,
            out_specs=(vmem, vmem),
            scratch_shapes=[
                pltpu.VMEM((video_count, 3, video_all, HEAD), half),
                pltpu.VMEM((cross_count, near * video_local, HEAD), half),
                pltpu.VMEM((cross_count, 2, audio_all, HEAD), half),
                pltpu.VMEM((audio_count, 3, audio_all, HEAD), half),
                pltpu.VMEM((across_count, audio_all, HEAD), half),
                pltpu.VMEM((across_count, 2, near * video_local, HEAD), half),
                pltpu.VMEM((video_count, video_all, HEAD), half),
                pltpu.VMEM((cross_count, near * video_local, HEAD), half),
                pltpu.VMEM((audio_count, audio_all, HEAD), half),
                pltpu.VMEM((across_count, audio_all, HEAD), half),
                pltpu.VMEM((across_count, audio_all // HEAD, 1, HEAD), jnp.float32),
                pltpu.VMEM(video_cross_q.shape, half),
                pltpu.VMEM(video_cross_q.shape, half),
                pltpu.VMEM(audio_cross_q.shape, half),
                pltpu.VMEM((2,) + audio_cross_q.shape, half),
                pltpu.VMEM((2 * branches * HA, 1, HEAD), jnp.float32),
                pltpu.VMEM((2, HEAD, branches * HA), jnp.float32),
                pltpu.SemaphoreType.DMA((video_count,)),
                pltpu.SemaphoreType.DMA((cross_count, 2)),
                pltpu.SemaphoreType.DMA((audio_count,)),
                pltpu.SemaphoreType.DMA((across_count, 2)),
                pltpu.SemaphoreType.DMA((11,)),
                pltpu.SemaphoreType.DMA((5,)),
            ],
            compiler_params=pltpu.CompilerParams(
                collective_id=0, has_side_effects=True, vmem_limit_bytes=52 * 2**20
            ),
        )(
            kinds_first(video_qkv),
            video_cross_q,
            kinds_first(audio_kv_v),
            kinds_first(audio_qkv),
            audio_cross_q,
            kinds_first(video_kv_a),
            video_gates.reshape(branches, 1, -1),
            audio_gates.reshape(branches * HA, 1, HEAD),
            bias.reshape(branches, 1, audio_all),
        )
    )


def solution(mesh):
    placed = (
        P("groups", "seq", None, None),
        P("groups", "seq", None),
        P("groups", "seq", None, None),
        P("groups", "seq", None, None),
        P("groups", "seq", None),
        P("groups", "seq", None, None),
        P("groups"),
        P("groups"),
        P(),
        P(),
    )
    return jax.shard_map(
        functools.partial(on_device, mesh.shape["seq"]),
        mesh=mesh,
        in_specs=placed,
        out_specs=(P("groups", "seq", None), P("groups", "seq", None)),
        check_vma=False,
    )
```

```python
import functools

import jax
import jax.numpy as jnp
from jax import lax
from jax.experimental import pallas as pl
from jax.experimental.pallas import tpu as pltpu
from jax.sharding import PartitionSpec as P

HV = 32
HA = 16
HEAD = 128
PROMPTS = 4
MESH = pl.DeviceIdType.MESH


def attend(queries, key_rows, value_rows, bias):
    scores = lax.dot_general(
        queries, key_rows, (((1,), (1,)), ((), ())), preferred_element_type=jnp.float32
    ) * (HEAD**-0.5)
    if bias is not None:
        scores = scores + bias
    row_max = jnp.max(scores, axis=1, keepdims=True)
    weights = jnp.exp(scores - row_max)
    total = jnp.sum(weights, axis=1, keepdims=True)
    result = jnp.dot(
        weights.astype(jnp.bfloat16), value_rows, preferred_element_type=jnp.float32
    )
    return result / total, row_max + jnp.log(total)


def block_kernel(
    n,
    video_count,
    cross_count,
    audio_count,
    across_count,
    video_block,
    audio_block,
    video_qkv,
    video_q,
    audio_kv,
    audio_qkv,
    audio_q,
    video_kv,
    video_gate,
    audio_gate,
    audio_valid,
    branch_prompt,
    video_out,
    audio_out,
    video_qkv_in,
    video_q_in,
    audio_kv_in,
    audio_qkv_in,
    audio_q_in,
    video_kv_in,
    video_res,
    cross_res,
    audio_res,
    across_res,
    level_res,
    own_home,
    cross_home,
    audio_home,
    across_home,
    level_home,
    share_mat,
    video_sems,
    cross_sems,
    audio_sems,
    across_sems,
    send_sems,
    back_sems,
):
    me = lax.axis_index("seq")
    group = lax.axis_index("groups")
    video_local = video_out.shape[1]
    audio_local = audio_out.shape[1]

    barrier = pltpu.get_barrier_semaphore()

    def greet(k, carry):
        peer = lax.rem(me + k, n)
        pl.semaphore_signal(barrier, inc=1, device_id=(group, peer), device_id_type=MESH)
        return carry

    lax.fori_loop(1, n, greet, 0)
    pl.semaphore_wait(barrier, n - 1)

    video_rows = pl.ds(pl.multiple_of(me * video_local, video_local), video_local)
    audio_rows = pl.ds(pl.multiple_of(me * audio_local, audio_local), audio_local)

    near = n // 2
    half_first = (me // near) * near
    place_in_half = me - half_first
    half_rows = pl.ds(pl.multiple_of(place_in_half * video_local, video_local), video_local)

    def columns(head):
        return pl.ds(pl.multiple_of(head * HEAD, HEAD), HEAD)

    def video_parts(item, slot):
        branch, head = item // HV, lax.rem(item, HV)
        return (
            (
                video_qkv.at[branch, :, :, columns(head)],
                video_qkv_in.at[slot, :, video_rows],
                video_sems.at[slot],
            ),
        )

    def cross_q_parts(item, slot):
        branch, head = item // HV, lax.rem(item, HV)
        return (
            (
                video_q.at[branch, :, columns(head)],
                video_q_in.at[slot, half_rows],
                cross_sems.at[slot, 0],
            ),
        )

    def cross_kv_parts(item, slot):
        branch, head = item // HV, lax.rem(item, HV)
        return (
            (
                audio_kv.at[branch, :, :, columns(head)],
                audio_kv_in.at[slot, :, audio_rows],
                cross_sems.at[slot, 1],
            ),
        )

    def audio_parts(item, slot):
        branch, head = item // HA, lax.rem(item, HA)
        return (
            (
                audio_qkv.at[branch, :, :, columns(head)],
                audio_qkv_in.at[slot, :, audio_rows],
                audio_sems.at[slot],
            ),
        )

    def across_q_parts(item, slot):
        branch, head = item // HA, lax.rem(item, HA)
        return (
            (
                audio_q.at[branch, :, columns(head)],
                audio_q_in.at[slot, audio_rows],
                across_sems.at[slot, 0],
            ),
        )

    def across_kv_parts(item, slot):
        branch, head = item // HA, lax.rem(item, HA)
        return (
            (
                video_kv.at[branch, :, :, columns(head)],
                video_kv_in.at[slot, :, half_rows],
                across_sems.at[slot, 1],
            ),
        )

    def send(parts, count, slot, first_sem, first, span, ring):
        def items_of(peer):
            return parts(lax.rem(peer, ring) * count + slot, slot)

        def to_peer(k, carry):
            step = k // 2 + lax.rem(k, 2) * (span // 2)
            peer = first + lax.rem(me - first + step, span)
            for place, (source, target, sem) in enumerate(items_of(peer)):
                pltpu.make_async_remote_copy(
                    src_ref=source,
                    dst_ref=target,
                    send_sem=send_sems.at[first_sem + place],
                    recv_sem=sem,
                    device_id=(group, peer),
                    device_id_type=MESH,
                ).start()
            return carry

        lax.fori_loop(1, span, to_peer, 0)
        for source, target, sem in items_of(me):
            pltpu.make_async_copy(source, target, sem).start()

    per_video = cross_count // (video_count - audio_count)
    per_audio = across_count // audio_count

    def send_video(slot, carry):
        send(video_parts, video_count, slot, 0, 0, n, n)
        return carry

    def send_crosses(slot, carry):
        first = (slot - audio_count) * per_video

        def send_cross(j, inner):
            send(cross_kv_parts, cross_count, first + j, 2, 0, n, near)
            send(cross_q_parts, cross_count, first + j, 1, half_first, near, near)
            return inner

        lax.fori_loop(0, per_video, send_cross, 0)
        return carry

    def send_audio(slot, carry):
        send(audio_parts, audio_count, slot, 3, 0, n, n)

        def send_across(j, inner):
            send(across_q_parts, across_count, slot * per_audio + j, 4, 0, n, near)
            send(across_kv_parts, across_count, slot * per_audio + j, 5, half_first, near, near)
            return inner

        lax.fori_loop(0, per_audio, send_across, 0)
        return carry

    def early(slot, carry, video, other):
        video(slot, carry)
        return other(slot, carry)

    lax.fori_loop(
        0, audio_count, functools.partial(early, video=send_video, other=send_audio), 0
    )
    lax.fori_loop(
        audio_count,
        video_count,
        functools.partial(early, video=send_video, other=send_crosses),
        0,
    )

    def mask(branch):
        positions = lax.broadcasted_iota(jnp.int32, (1, audio_kv_in.shape[2]), 1)
        return jnp.where(positions < audio_valid[branch], 0.0, -jnp.inf)

    def gate_of(gates, branch, here):
        return sum(
            (branch_prompt[branch] == p).astype(jnp.int32).astype(jnp.float32)
            * gates[p : p + 1, here]
            for p in range(PROMPTS)
        )

    def settle(ref, sem):
        pltpu.make_async_copy(ref, ref, sem).wait()

    def give_back(result, slot, out, branch, head, local, base, first, count, place):
        def to_peer(j, carry):
            peer = base + first + j
            source = result.at[slot, pl.ds(pl.multiple_of((first + j) * local, local), local)]
            target = out.at[branch, :, columns(head)]

            @pl.when(peer == me)
            def _():
                pltpu.make_async_copy(source, target, back_sems.at[place]).start()

            @pl.when(peer != me)
            def _():
                pltpu.make_async_remote_copy(
                    src_ref=source,
                    dst_ref=target,
                    send_sem=send_sems.at[6 + place],
                    recv_sem=back_sems.at[place],
                    device_id=(group, peer),
                    device_id_type=MESH,
                ).start()

            return carry

        lax.fori_loop(0, count, to_peer, 0)

    def video_item(slot, carry):
        item = me * video_count + slot
        branch, head = item // HV, lax.rem(item, HV)
        settle(video_qkv_in.at[slot], video_sems.at[slot])
        block = video_block * video_local

        def rows(i, inner):
            here = pl.ds(pl.multiple_of(i * block, block), block)
            own, _ = attend(
                video_qkv_in[slot, 0, here], video_qkv_in[slot, 1], video_qkv_in[slot, 2], None
            )
            video_res[slot, here] = own.astype(jnp.bfloat16)
            give_back(
                video_res, slot, own_home, branch, head, video_local, 0, i * video_block,
                video_block, 0,
            )
            return inner

        lax.fori_loop(0, n // video_block, rows, 0)
        return carry

    def cross_items(slot, carry):
        def cross(j, inner):
            cross_item((slot - audio_count) * per_video + j)
            return inner

        lax.fori_loop(0, per_video, cross, 0)
        return carry

    def cross_item(slot):
        item = place_in_half * cross_count + slot
        branch, head = item // HV, lax.rem(item, HV)
        settle(video_q_in.at[slot], cross_sems.at[slot, 0])
        settle(audio_kv_in.at[slot], cross_sems.at[slot, 1])
        block = video_block * video_local

        def rows(i, inner):
            here = pl.ds(pl.multiple_of(i * block, block), block)
            cross, _ = attend(
                video_q_in[slot, here], audio_kv_in[slot, 0], audio_kv_in[slot, 1], mask(branch)
            )
            cross_res[slot, here] = cross.astype(jnp.bfloat16)
            give_back(
                cross_res, slot, cross_home, branch, head, video_local, half_first,
                i * video_block, video_block, 2,
            )
            return inner

        lax.fori_loop(0, near // video_block, rows, 0)

    def audio_item(slot, carry):
        item = me * audio_count + slot
        branch, head = item // HA, lax.rem(item, HA)
        settle(audio_qkv_in.at[slot], audio_sems.at[slot])
        block = audio_block * audio_local

        def rows(i, inner):
            here = pl.ds(pl.multiple_of(i * block, block), block)
            own, _ = attend(
                audio_qkv_in[slot, 0, here],
                audio_qkv_in[slot, 1],
                audio_qkv_in[slot, 2],
                mask(branch),
            )
            audio_res[slot, here] = own.astype(jnp.bfloat16)
            give_back(
                audio_res, slot, audio_home, branch, head, audio_local, 0, i * audio_block,
                audio_block, 1,
            )
            return inner

        lax.fori_loop(0, n // audio_block, rows, 0)

        def across(j, inner):
            across_item(slot * per_audio + j)
            return inner

        lax.fori_loop(0, per_audio, across, 0)
        return carry

    my_half = me // near

    def across_item(slot):
        item = place_in_half * across_count + slot
        branch, head = item // HA, lax.rem(item, HA)
        settle(audio_q_in.at[slot], across_sems.at[slot, 0])
        settle(video_kv_in.at[slot], across_sems.at[slot, 1])
        block = audio_block * audio_local

        def rows(i, inner):
            here = pl.ds(pl.multiple_of(i * block, block), block)
            part, level = attend(
                audio_q_in[slot, here], video_kv_in[slot, 0], video_kv_in[slot, 1], None
            )
            across_res[slot, here] = part.astype(jnp.bfloat16)
            for c in range(block // HEAD):
                column = jnp.broadcast_to(level[c * HEAD : (c + 1) * HEAD], (HEAD, HEAD))
                level_res[slot, i * (block // HEAD) + c] = jnp.transpose(column)[0:1]
            give_back(
                across_res, slot, across_home.at[my_half], branch, head, audio_local, 0,
                i * audio_block, audio_block, 3,
            )
            return inner

        lax.fori_loop(0, n // audio_block, rows, 0)

        def levels(k, inner):
            peer = lax.rem(me + k, n)
            pltpu.make_async_remote_copy(
                src_ref=level_res.at[slot, (peer * audio_local) // HEAD],
                dst_ref=level_home.at[my_half * (audio_home.shape[0] * HA) + item],
                send_sem=send_sems.at[10],
                recv_sem=back_sems.at[4],
                device_id=(group, peer),
                device_id_type=MESH,
            ).start()
            return inner

        lax.fori_loop(1, n, levels, 0)
        pltpu.make_async_copy(
            level_res.at[slot, (me * audio_local) // HEAD],
            level_home.at[my_half * (audio_home.shape[0] * HA) + item],
            back_sems.at[4],
        ).start()

    lax.fori_loop(
        0, audio_count, functools.partial(early, video=video_item, other=audio_item), 0
    )
    lax.fori_loop(
        audio_count,
        video_count,
        functools.partial(early, video=video_item, other=cross_items),
        0,
    )

    settle(audio_home, back_sems.at[1])
    settle(across_home, back_sems.at[3])
    settle(level_home, back_sems.at[4])
    items = level_home.shape[0] // 2
    low, high = level_home[:items, 0], level_home[items:, 0]
    for place, gap in enumerate((high - low, low - high)):
        share_mat[place] = jnp.transpose(1.0 / (1.0 + jnp.exp(gap)))
    mine = pl.ds(pl.multiple_of(lax.rem(me * audio_local, HEAD), audio_local), audio_local)
    low_share, high_share = share_mat[0, mine], share_mat[1, mine]
    for item in range(low_share.shape[1]):
        branch, head = item // HA, item % HA
        here = slice(head * HEAD, (head + 1) * HEAD)
        across = (
            low_share[:, item : item + 1] * across_home[0, branch, :, here].astype(jnp.float32)
            + high_share[:, item : item + 1] * across_home[1, branch, :, here].astype(jnp.float32)
        )
        audio_out[branch, :, here] = (
            audio_home[branch, :, here].astype(jnp.float32) + gate_of(audio_gate, branch, here) * across
        ).astype(jnp.bfloat16)

    settle(own_home, back_sems.at[0])
    settle(cross_home, back_sems.at[2])
    width = 512

    def combine(i, carry):
        here = pl.ds(pl.multiple_of(i * width, width), width)
        for branch in range(own_home.shape[0]):
            video_out[branch, :, here] = (
                own_home[branch, :, here].astype(jnp.float32)
                + gate_of(video_gate, branch, here) * cross_home[branch, :, here].astype(jnp.float32)
            ).astype(jnp.bfloat16)
        return carry

    lax.fori_loop(0, video_out.shape[2] // width, combine, 0)

    far_video = pl.ds(0, (n - 1) * video_local)
    far_audio = pl.ds(0, (n - 1) * audio_local)
    far_half = pl.ds(0, (near - 1) * video_local)
    settle(video_qkv_in.at[:, :, far_video], send_sems.at[0])
    settle(video_q_in.at[:, far_half], send_sems.at[1])
    settle(audio_kv_in.at[:, :, far_audio], send_sems.at[2])
    settle(audio_qkv_in.at[:, :, far_audio], send_sems.at[3])
    settle(audio_q_in.at[:, far_audio], send_sems.at[4])
    settle(video_kv_in.at[:, :, far_half], send_sems.at[5])
    settle(video_res.at[:, far_video], send_sems.at[6])
    settle(audio_res.at[:, far_audio], send_sems.at[7])
    settle(cross_res.at[:, far_half], send_sems.at[8])
    settle(across_res.at[:, far_audio], send_sems.at[9])
    settle(level_home.at[pl.ds(0, across_count * (n - 1))], send_sems.at[10])


def kinds_first(source):
    return jnp.transpose(source, (0, 2, 1, 3))


def on_device(
    n,
    video_qkv,
    video_cross_q,
    audio_kv_v,
    audio_qkv,
    audio_cross_q,
    video_kv_a,
    audio_valid,
    branch_prompt,
    video_gate,
    audio_gate,
):
    branches, video_local = video_cross_q.shape[:2]
    audio_local = audio_cross_q.shape[1]
    video_all, audio_all = video_local * n, audio_local * n
    video_count, audio_count = branches * HV // n, branches * HA // n
    near = n // 2
    cross_count, across_count = branches * HV // near, branches * HA // near
    hbm = pl.BlockSpec(memory_space=pl.ANY)
    vmem = pl.BlockSpec(memory_space=pltpu.VMEM)
    smem = pl.BlockSpec(memory_space=pltpu.SMEM)
    half = jnp.bfloat16
    return tuple(
        pl.pallas_call(
            functools.partial(
                block_kernel, n, video_count, cross_count, audio_count, across_count, min(4, near), min(8, n)
            ),
            out_shape=(
                jax.ShapeDtypeStruct(video_cross_q.shape, half),
                jax.ShapeDtypeStruct(audio_cross_q.shape, half),
            ),
            in_specs=[hbm] * 6 + [vmem] * 2 + [smem] * 2,
            out_specs=(vmem, vmem),
            scratch_shapes=[
                pltpu.VMEM((video_count, 3, video_all, HEAD), half),
                pltpu.VMEM((cross_count, near * video_local, HEAD), half),
                pltpu.VMEM((cross_count, 2, audio_all, HEAD), half),
                pltpu.VMEM((audio_count, 3, audio_all, HEAD), half),
                pltpu.VMEM((across_count, audio_all, HEAD), half),
                pltpu.VMEM((across_count, 2, near * video_local, HEAD), half),
                pltpu.VMEM((video_count, video_all, HEAD), half),
                pltpu.VMEM((cross_count, near * video_local, HEAD), half),
                pltpu.VMEM((audio_count, audio_all, HEAD), half),
                pltpu.VMEM((across_count, audio_all, HEAD), half),
                pltpu.VMEM((across_count, audio_all // HEAD, 1, HEAD), jnp.float32),
                pltpu.VMEM(video_cross_q.shape, half),
                pltpu.VMEM(video_cross_q.shape, half),
                pltpu.VMEM(audio_cross_q.shape, half),
                pltpu.VMEM((2,) + audio_cross_q.shape, half),
                pltpu.VMEM((2 * branches * HA, 1, HEAD), jnp.float32),
                pltpu.VMEM((2, HEAD, branches * HA), jnp.float32),
                pltpu.SemaphoreType.DMA((video_count,)),
                pltpu.SemaphoreType.DMA((cross_count, 2)),
                pltpu.SemaphoreType.DMA((audio_count,)),
                pltpu.SemaphoreType.DMA((across_count, 2)),
                pltpu.SemaphoreType.DMA((11,)),
                pltpu.SemaphoreType.DMA((5,)),
            ],
            compiler_params=pltpu.CompilerParams(
                collective_id=0, has_side_effects=True, vmem_limit_bytes=52 * 2**20
            ),
        )(
            kinds_first(video_qkv),
            video_cross_q,
            kinds_first(audio_kv_v),
            kinds_first(audio_qkv),
            audio_cross_q,
            kinds_first(video_kv_a),
            video_gate,
            audio_gate,
            audio_valid,
            branch_prompt,
        )
    )


def solution(mesh):
    placed = (
        P("groups", "seq", None, None),
        P("groups", "seq", None),
        P("groups", "seq", None, None),
        P("groups", "seq", None, None),
        P("groups", "seq", None),
        P("groups", "seq", None, None),
        P("groups"),
        P("groups"),
        P(),
        P(),
    )
    return jax.shard_map(
        functools.partial(on_device, mesh.shape["seq"]),
        mesh=mesh,
        in_specs=placed,
        out_specs=(P("groups", "seq", None), P("groups", "seq", None)),
        check_vma=False,
    )
```
